32 devices in a mesh: tm: 8 (over z, x), chan: 4 (over y, core).
Axes of the slice: x: 2, y: 2, z: 4, core: 2. Of those that a mesh axis runs over, the one named last changes fastest.
Arguments:
- samples: bfloat16 [4096, 16384], P('tm', 'chan'), may hold values from -180 to 180
- sketch: bfloat16 [16384, 512], P('chan'), may hold values from -0.046875 to 0.046875
Outputs:
- coords: float32 [4096, 512], P('tm')
- weights: float32 [4096], P('tm')
The draws below stay inside these ranges and needn't reach their ends.
All inputs are finite; a program needn't handle non-finite values.
Results may differ from the reference program's by a relative error of at most 0.0033.
Values may be sent and summed in bfloat16 or wider, within the bound.
A program may use at most 64 MiB of HBM per device.

```python
import math
import jax
import jax.numpy as jnp
from jax import lax

C = 16384
K = 512
ROUNDS = 2
SAMPLES = 4096


def draw_samples(key, part):
    first_key, second_key = jax.random.split(key)
    noise_part = jax.random.truncated_normal(first_key, -5.0, 5.0, (SAMPLES, C))
    low_end = 0.5
    high_end = 4.0
    row_scale = jnp.exp(jax.random.uniform(second_key, (SAMPLES, 1), minval=math.log(low_end), maxval=math.log(high_end)))
    time_rise = 1.0 + 2.0 * jnp.arange(SAMPLES, dtype=jnp.float32)[:, None] / (SAMPLES - 1)
    chan_rise = 1.0 + 2.0 * jnp.arange(C, dtype=jnp.float32)[None, :] / (C - 1)
    return (noise_part * row_scale * time_rise * chan_rise).astype(jnp.bfloat16)


def block_levels(key, extent, cuts, least, high):
    def one(axis_at, parts):
        draws = jax.random.uniform(jax.random.fold_in(jax.random.fold_in(key, 6), axis_at), (parts,), jnp.float32, least / len(cuts), high / len(cuts))
        return jnp.repeat(jnp.exp(draws), extent[axis_at] // parts).reshape((-1,) + (1,) * (len(extent) - axis_at - 1))

    factor_of = one(*cuts[0])
    for cut in cuts[1:]:
        factor_of = factor_of * one(*cut)
    return factor_of


def scatter_about(stream_key, shape, deviation, bound, shards=(), held_as=jnp.bfloat16):
    drawn = deviation * jax.random.normal(stream_key, shape, jnp.float32)
    if shards:
        drawn = drawn * block_levels(stream_key, shape, shards, -0.22, 0.18)
    return jnp.clip(drawn, -bound, bound).astype(held_as)


def setup_inputs(seed: int = 0) -> dict:
    streams_of = jax.random.split(jax.random.key(seed), 3)
    samples = draw_samples(jax.random.fold_in(streams_of[2], 71), 0)
    sketch = scatter_about(streams_of[1], (C, K), C ** -0.5, 0.046875, ((0, 4),))
    return dict(samples=samples, sketch=sketch)


def reference(samples, sketch):
    sketched = jnp.dot(samples.astype(jnp.float32), sketch.astype(jnp.float32), preferred_element_type=jnp.float32)
    weights = jnp.ones((samples.shape[0],), jnp.float32)
    coords = jnp.zeros((samples.shape[0], sketch.shape[1]), jnp.float32)
    for step in range(ROUNDS):
        weighted = ((weights * weights)[:, None] * sketched).astype(jnp.bfloat16)
        factor = jnp.dot(samples.T.astype(jnp.float32), weighted.astype(jnp.float32), preferred_element_type=jnp.float32)
        gram = jnp.dot(factor.T.astype(jnp.float32), factor.astype(jnp.float32), precision=lax.Precision.HIGHEST, preferred_element_type=jnp.float32)
        lower = jnp.linalg.cholesky(gram)
        basis = lax.linalg.triangular_solve(lower, factor, left_side=False, lower=True, transpose_a=True).astype(jnp.bfloat16)
        coords = jnp.dot(samples.astype(jnp.float32), basis.astype(jnp.float32), preferred_element_type=jnp.float32)
        back = jnp.dot(coords.astype(jnp.bfloat16).astype(jnp.float32), basis.T.astype(jnp.float32), preferred_element_type=jnp.float32)
        resid = samples.astype(jnp.float32) - back
        energy = lax.optimization_barrier(jnp.sum(resid * resid, axis=1))
        weights = jnp.minimum(1.0, 3.0 / jnp.sqrt(energy / C + 1e-06))
    return (coords, weights)
```

```python
import jax
import jax.numpy as jnp
from jax import lax
from jax.sharding import PartitionSpec as P

ROUNDS = 2


def shards(samples, sketch, channels):
    rows, rank = samples.shape[0], sketch.shape[1]
    f32 = jnp.float32
    wide = samples.astype(f32)
    norms = jnp.sum(wide * wide, axis=1)
    local = jnp.dot(samples, sketch, preferred_element_type=f32)
    both = jnp.concatenate([local, jnp.broadcast_to(norms[:, None], (rows, 128))], axis=1)
    both = lax.psum(both, "chan")
    sketched, norms = both[:, :rank], both[:, rank]
    weights = jnp.ones((rows,), f32)
    for step in range(ROUNDS):
        weighted = ((weights * weights)[:, None] * sketched).astype(jnp.bfloat16)
        local_factor = jnp.einsum("sc,sk->ck", samples, weighted, preferred_element_type=f32)
        part = lax.psum_scatter(local_factor.astype(jnp.bfloat16), "tm", scatter_dimension=0, tiled=True)
        factor = lax.all_gather(part, "tm", axis=0, tiled=True)
        gram = jnp.einsum("ck,cl->kl", factor, factor, preferred_element_type=f32)
        seen = jnp.dot(samples, factor, preferred_element_type=f32)
        both = lax.psum(jnp.concatenate([gram, seen], axis=0), "chan")
        gram, seen = both[:rank], both[rank:]
        lower = jnp.linalg.cholesky(gram)
        coords = lax.linalg.triangular_solve(lower, seen, left_side=False, lower=True, transpose_a=True)
        energy = jnp.maximum(norms - jnp.sum(coords * coords, axis=1), 0.0)
        weights = jnp.minimum(1.0, 3.0 / jnp.sqrt(energy / channels + 1e-06))
    return (coords, weights)


def solution(mesh):
    in_specs = (P("tm", "chan"), P("chan", None))
    out_specs = (P("tm", None), P("tm"))

    def whole(samples, sketch):
        f = lambda a, b: shards(a, b, samples.shape[1])
        return jax.shard_map(f, mesh=mesh, in_specs=in_specs, out_specs=out_specs, check_vma=False)(samples, sketch)

    return whole
```

```python
import functools

import jax
import jax.numpy as jnp
from jax import lax
from jax.experimental import pallas as pl
from jax.experimental.pallas import tpu as pltpu
from jax.sharding import PartitionSpec as P

ROUNDS = 2
B = 128
HIGH = lax.Precision.HIGHEST


def dot_t(a, b):
    return lax.dot_general(a, b, (((1,), (1,)), ((), ())), precision=HIGH, preferred_element_type=jnp.float32)


def invert_block(block, inv_ref):
    eye = lax.broadcasted_iota(jnp.int32, (B, B), 0) == lax.broadcasted_iota(jnp.int32, (B, B), 1)
    left, right = block, eye.astype(jnp.float32)
    top = 0
    for j in range(B):
        cut = (j // 8) * 8 - top
        if cut:
            left, right, top = left[cut:], right[cut:], top + cut
        k = j - top
        scale = lax.rsqrt(left[k : k + 1, j : j + 1])
        row_left = left[k : k + 1, :] * scale
        row_right = right[k : k + 1, :] * scale
        inv_ref[j : j + 1, :] = row_right
        if j + 1 < B:
            col = left[:, j : j + 1] * scale
            left = left - col * row_left
            right = right - col * row_right


def fit_kernel(channels, both_ref, sketched_ref, norms_ref, coords_ref, weights_ref, weighted_ref, work, inv):
    rank = coords_ref.shape[1]
    total = work.shape[0]
    work[...] = both_ref[...]

    def block_step(b, carry):
        at = pl.multiple_of(b * B, B)
        invert_block(work[pl.ds(at, B), pl.ds(at, B)], inv)
        for k in range(rank // B):

            @pl.when(b == k)
            def _():
                lo, hi = k * B, (k + 1) * B
                panel = dot_t(work[hi:, lo:hi], inv[...])
                coords_ref[:, lo:hi] = panel[rank - hi :]
                if hi < rank:
                    work[hi:, hi:] = work[hi:, hi:] - dot_t(panel, panel[: rank - hi])

        return carry

    lax.fori_loop(0, rank // B, block_step, 0)
    coords = coords_ref[...]
    energy = jnp.maximum(norms_ref[:, :1] - jnp.sum(coords * coords, axis=1, keepdims=True), 0.0)
    weights = jnp.minimum(1.0, 3.0 / jnp.sqrt(energy / channels + 1e-06))
    weights_ref[...] = weights
    weighted_ref[...] = ((weights * weights) * sketched_ref[...]).astype(jnp.bfloat16)


def fit(channels, both, sketched, norms):
    rows, rank = sketched.shape
    return pl.pallas_call(
        functools.partial(fit_kernel, channels),
        out_shape=(
            jax.ShapeDtypeStruct((rows, rank), jnp.float32),
            jax.ShapeDtypeStruct((rows, 1), jnp.float32),
            jax.ShapeDtypeStruct((rows, rank), jnp.bfloat16),
        ),
        scratch_shapes=[pltpu.VMEM(both.shape, jnp.float32), pltpu.VMEM((B, B), jnp.float32)],
        compiler_params=pltpu.CompilerParams(vmem_limit_bytes=32 * 1024 * 1024),
    )(both, sketched, norms)


def shards(samples, sketch, channels):
    rows, rank = samples.shape[0], sketch.shape[1]
    f32 = jnp.float32
    wide = samples.astype(f32)
    norms = jnp.sum(wide * wide, axis=1)
    local = jnp.dot(samples, sketch, preferred_element_type=f32)
    both = jnp.concatenate([local, jnp.broadcast_to(norms[:, None], (rows, 128))], axis=1)
    both = lax.psum(both, "chan")
    sketched, norms = both[:, :rank], both[:, rank:]
    weighted = sketched.astype(jnp.bfloat16)
    for step in range(ROUNDS):
        local_factor = jnp.einsum("sc,sk->ck", samples, weighted, preferred_element_type=f32)
        part = lax.psum_scatter(local_factor.astype(jnp.bfloat16), "tm", scatter_dimension=0, tiled=True)
        factor = lax.all_gather(part, "tm", axis=0, tiled=True)
        gram = jnp.einsum("ck,cl->kl", factor, factor, preferred_element_type=f32)
        seen = jnp.dot(samples, factor, preferred_element_type=f32)
        both = lax.psum(jnp.concatenate([gram, seen], axis=0), "chan")
        coords, weights, weighted = fit(channels, both, sketched, norms)
    return (coords, weights[:, 0])


def solution(mesh):
    in_specs = (P("tm", "chan"), P("chan", None))
    out_specs = (P("tm", None), P("tm"))

    def whole(samples, sketch):
        f = lambda a, b: shards(a, b, samples.shape[1])
        return jax.shard_map(f, mesh=mesh, in_specs=in_specs, out_specs=out_specs, check_vma=False)(samples, sketch)

    return whole
```

```python
import functools

import jax
import jax.numpy as jnp
from jax import lax
from jax.experimental import pallas as pl
from jax.experimental.pallas import tpu as pltpu
from jax.sharding import PartitionSpec as P

ROUNDS = 2
B = 128
HIGH = lax.Precision.HIGHEST
MESH = pl.DeviceIdType.MESH


def dot_t(a, b):
    return lax.dot_general(a, b, (((1,), (1,)), ((), ())), precision=HIGH, preferred_element_type=jnp.float32)


def invert_block(block, inv_ref):
    eye = lax.broadcasted_iota(jnp.int32, (B, B), 0) == lax.broadcasted_iota(jnp.int32, (B, B), 1)
    left, right = block, eye.astype(jnp.float32)
    top = 0
    for j in range(B):
        cut = (j // 8) * 8 - top
        if cut:
            left, right, top = left[cut:], right[cut:], top + cut
        k = j - top
        scale = lax.rsqrt(left[k : k + 1, j : j + 1])
        row_left = left[k : k + 1, :] * scale
        row_right = right[k : k + 1, :] * scale
        inv_ref[j : j + 1, :] = row_right
        if j + 1 < B:
            col = left[:, j : j + 1] * scale
            left = left - col * row_left
            right = right - col * row_right


def fit_kernel(channels, both_ref, sketched_ref, norms_ref, coords_ref, weights_ref, weighted_ref, work, inv):
    rank = coords_ref.shape[1]
    total = work.shape[0]
    work[...] = both_ref[...]

    def block_step(b, carry):
        at = pl.multiple_of(b * B, B)
        invert_block(work[pl.ds(at, B), pl.ds(at, B)], inv)
        for k in range(rank // B):

            @pl.when(b == k)
            def _():
                lo, hi = k * B, (k + 1) * B
                panel = dot_t(work[hi:, lo:hi], inv[...])
                coords_ref[:, lo:hi] = panel[rank - hi :]
                if hi < rank:
                    work[hi:, hi:] = work[hi:, hi:] - dot_t(panel, panel[: rank - hi])

        return carry

    lax.fori_loop(0, rank // B, block_step, 0)
    coords = coords_ref[...]
    energy = jnp.maximum(norms_ref[:, :1] - jnp.sum(coords * coords, axis=1, keepdims=True), 0.0)
    weights = jnp.minimum(1.0, 3.0 / jnp.sqrt(energy / channels + 1e-06))
    weights_ref[...] = weights
    weighted_ref[...] = ((weights * weights) * sketched_ref[...]).astype(jnp.bfloat16)


def fit(channels, both, sketched, norms):
    rows, rank = sketched.shape
    return pl.pallas_call(
        functools.partial(fit_kernel, channels),
        out_shape=(
            jax.ShapeDtypeStruct((rows, rank), jnp.float32),
            jax.ShapeDtypeStruct((rows, 1), jnp.float32),
            jax.ShapeDtypeStruct((rows, rank), jnp.bfloat16),
        ),
        scratch_shapes=[pltpu.VMEM(both.shape, jnp.float32), pltpu.VMEM((B, B), jnp.float32)],
        compiler_params=pltpu.CompilerParams(vmem_limit_bytes=32 * 1024 * 1024),
    )(both, sketched, norms)


def exchange_kernel(outer, inner, mine_ref, samples_ref, both_ref, whole, near, sent, far, acc, near_sem, far_sem, wide_sem, local_sem):
    me = lax.axis_index("tm")
    o, i = me // inner, me % inner
    size, rank = acc.shape
    f32 = jnp.float32

    def peer_in(d):
        return {"tm": o * inner + (i + d) % inner}

    def peer_out(e):
        return {"tm": ((o + e) % outer) * inner + i}

    barrier = pltpu.get_barrier_semaphore()
    for d in range(1, inner):
        pl.semaphore_signal(barrier, inc=1, device_id=peer_in(d), device_id_type=MESH)
    for e in range(1, outer):
        pl.semaphore_signal(barrier, inc=1, device_id=peer_out(e), device_id_type=MESH)
    pl.semaphore_wait(barrier, inner + outer - 2)

    def copy(src, dst, sems, at, device):
        return pltpu.make_async_remote_copy(
            src_ref=src,
            dst_ref=dst,
            send_sem=sems.at[(0,) + at],
            recv_sem=sems.at[(1,) + at],
            device_id=device,
            device_id_type=MESH,
        )

    order = list(range(1, outer)) + [0]
    first = {}
    for e in order:
        row = (o + e) % outer
        for d in range(1, inner):
            block = row * inner + (i + d) % inner
            first[e, d] = copy(mine_ref.at[block], near.at[e, d - 1], near_sem, (e, d - 1), peer_in(d))
            first[e, d].start()
    second = {}
    for e in order:
        for d in range(1, inner):
            first[e, d].wait_recv()
        total = mine_ref[((o + e) % outer) * inner + i].astype(f32)
        for d in range(1, inner):
            total = total + near[e, d - 1].astype(f32)
        if e:
            sent[e - 1] = total.astype(jnp.bfloat16)
            second[e] = copy(sent.at[e - 1], far.at[e - 1], far_sem, (e - 1,), peer_out(e))
            second[e].start()
        else:
            acc[...] = total
    for e in range(1, outer):
        second[e].wait_recv()
        acc[...] = acc[...] + far[e - 1].astype(f32)
    whole[me] = acc[...].astype(jnp.bfloat16)

    def wide(e):
        return copy(whole.at[me], whole.at[me], wide_sem, (e - 1,), peer_out(e))

    def local(e, d):
        block = ((o - e + outer) % outer) * inner + i
        return copy(whole.at[block], whole.at[block], local_sem, (e, d - 1), peer_in(d))

    for e in range(1, outer):
        wide(e).start()
    for d in range(1, inner):
        local(0, d).start()
    both_ref[...] = jnp.zeros_like(both_ref)

    def use(block):
        part = whole[block]
        columns = pl.ds(pl.multiple_of(block * size, size), size)
        both_ref[:rank] += lax.dot_general(part, part, (((0,), (0,)), ((), ())), preferred_element_type=f32)
        both_ref[rank:] += jnp.dot(samples_ref[:, columns], part, preferred_element_type=f32)

    use(me)
    for e in range(1, outer):
        block = ((o - e + outer) % outer) * inner + i
        copy(whole.at[block], whole.at[block], wide_sem, (e - 1,), peer_out(e)).wait_recv()
        for d in range(1, inner):
            local(e, d).start()
        use(block)
    for e in range(outer):
        for d in range(1, inner):
            block = ((o - e + outer) % outer) * inner + (i - d + inner) % inner
            copy(whole.at[block], whole.at[block], local_sem, (e, d - 1), peer_in(d)).wait_recv()
            use(block)
    for one in first.values():
        one.wait_send()
    for one in second.values():
        one.wait_send()
    for e in range(1, outer):
        wide(e).wait_send()
    for e in range(outer):
        for d in range(1, inner):
            local(e, d).wait_send()


def exchange(mine, samples, devices):
    rows, channels = samples.shape
    rank = mine.shape[1]
    outer = 4 if devices % 4 == 0 else 1
    inner = devices // outer
    size = channels // devices
    low = jnp.bfloat16
    return pl.pallas_call(
        functools.partial(exchange_kernel, outer, inner),
        out_shape=jax.ShapeDtypeStruct((rank + rows, rank), jnp.float32),
        in_specs=[pl.BlockSpec(memory_space=pltpu.VMEM)] * 2,
        out_specs=pl.BlockSpec(memory_space=pltpu.VMEM),
        scratch_shapes=[
            pltpu.VMEM((devices, size, rank), low),
            pltpu.VMEM((outer, inner - 1, size, rank), low),
            pltpu.VMEM((outer - 1, size, rank), low),
            pltpu.VMEM((outer - 1, size, rank), low),
            pltpu.VMEM((size, rank), jnp.float32),
            pltpu.SemaphoreType.DMA((2, outer, inner - 1)),
            pltpu.SemaphoreType.DMA((2, outer - 1)),
            pltpu.SemaphoreType.DMA((2, outer - 1)),
            pltpu.SemaphoreType.DMA((2, outer, inner - 1)),
        ],
        compiler_params=pltpu.CompilerParams(
            collective_id=0, has_side_effects=True, vmem_limit_bytes=40 * 1024 * 1024
        ),
    )(mine.reshape(devices, size, rank), samples)


def shards(samples, sketch, channels, devices):
    rows, rank = samples.shape[0], sketch.shape[1]
    f32 = jnp.float32
    wide = samples.astype(f32)
    norms = jnp.sum(wide * wide, axis=1)
    local = jnp.dot(samples, sketch, preferred_element_type=f32)
    both = jnp.concatenate([local, jnp.broadcast_to(norms[:, None], (rows, 128))], axis=1)
    both = lax.psum(both, "chan")
    sketched, norms = both[:, :rank], both[:, rank:]
    weighted = sketched.astype(jnp.bfloat16)
    for step in range(ROUNDS):
        local_factor = jnp.einsum("sc,sk->ck", samples, weighted, preferred_element_type=f32)
        both = lax.psum(exchange(local_factor.astype(jnp.bfloat16), samples, devices), "chan")
        coords, weights, weighted = fit(channels, both, sketched, norms)
    return (coords, weights[:, 0])


def solution(mesh):
    in_specs = (P("tm", "chan"), P("chan", None))
    out_specs = (P("tm", None), P("tm"))

    def whole(samples, sketch):
        f = lambda a, b: shards(a, b, samples.shape[1], mesh.shape["tm"])
        return jax.shard_map(f, mesh=mesh, in_specs=in_specs, out_specs=out_specs, check_vma=False)(samples, sketch)

    return whole
```

```python
import functools

import jax
import jax.numpy as jnp
from jax import lax
from jax.experimental import pallas as pl
from jax.experimental.pallas import tpu as pltpu
from jax.sharding import PartitionSpec as P

ROUNDS = 2
B = 128
HIGH = lax.Precision.HIGHEST
MESH = pl.DeviceIdType.MESH


def dot_t(a, b):
    return lax.dot_general(a, b, (((1,), (1,)), ((), ())), precision=HIGH, preferred_element_type=jnp.float32)


def invert_block(block, inv_ref):
    eye = lax.broadcasted_iota(jnp.int32, (B, B), 0) == lax.broadcasted_iota(jnp.int32, (B, B), 1)
    left, right = block, eye.astype(jnp.float32)
    top = 0
    for j in range(B):
        cut = (j // 8) * 8 - top
        if cut:
            left, right, top = left[cut:], right[cut:], top + cut
        k = j - top
        scale = lax.rsqrt(left[k : k + 1, j : j + 1])
        row_left = left[k : k + 1, :] * scale
        row_right = right[k : k + 1, :] * scale
        inv_ref[j : j + 1, :] = row_right
        if j + 1 < B:
            col = left[:, j : j + 1] * scale
            left = left - col * row_left
            right = right - col * row_right


def copier(sems, axis, count):
    me = lax.axis_index(axis)

    def copy(slot, d, src, dst):
        return pltpu.make_async_remote_copy(
            src_ref=src,
            dst_ref=dst,
            send_sem=sems.at[0, slot, d - 1],
            recv_sem=sems.at[1, slot, d - 1],
            device_id={axis: (me + d) % count},
            device_id_type=MESH,
        )

    return copy


def greet(axis, count):
    me = lax.axis_index(axis)
    barrier = pltpu.get_barrier_semaphore()
    for d in range(1, count):
        pl.semaphore_signal(barrier, inc=1, device_id={axis: (me + d) % count}, device_id_type=MESH)
    pl.semaphore_wait(barrier, count - 1)


def part(index, size, base=0):
    return pl.ds(pl.multiple_of(base + index * size, size), size)


def scatter_copies(copy, slot, count, source, base, size, slots):
    me = lax.axis_index("chan")
    return [
        copy(slot, d, source.at[part((me + d) % count, size, base)], slots.at[d - 1]) for d in range(1, count)
    ]


def gather_rows(copy, slot, count, whole, size):
    me = lax.axis_index("chan")
    sends = [copy(slot, d, whole.at[part(me, size)], whole.at[part(me, size)]) for d in range(1, count)]
    for one in sends:
        one.start()
    for d in range(1, count):
        came = whole.at[part((me - d + count) % count, size)]
        copy(slot, d, came, came).wait_recv()
    for one in sends:
        one.wait_send()


def start_kernel(count, local_ref, own_ref, weighted_ref, slots, gathered, sems):
    size, rank = slots.shape[1], weighted_ref.shape[1]
    me = lax.axis_index("chan")
    greet("chan", count)
    copy = copier(sems, "chan", count)
    sends = scatter_copies(copy, 0, count, local_ref, 0, size, slots)
    for one in sends:
        one.start()
    total = local_ref[part(me, size)]
    for one in sends:
        one.wait_recv()
    for d in range(1, count):
        total = total + slots[d - 1]
    own_ref[...] = total
    gathered[part(me, size)] = total[:, :rank].astype(jnp.bfloat16)
    gather_rows(copy, 1, count, gathered, size)
    for one in sends:
        one.wait_send()
    weighted_ref[...] = gathered[...]


def start(local, rank, count):
    rows, wide = local.shape
    size = rows // count
    return pl.pallas_call(
        functools.partial(start_kernel, count),
        out_shape=(
            jax.ShapeDtypeStruct((size, wide), jnp.float32),
            jax.ShapeDtypeStruct((rows, rank), jnp.bfloat16),
        ),
        scratch_shapes=[
            pltpu.VMEM((count - 1, size, wide), jnp.float32),
            pltpu.VMEM((rows, rank), jnp.bfloat16),
            pltpu.SemaphoreType.DMA((2, 2, count - 1)),
        ],
        compiler_params=pltpu.CompilerParams(
            collective_id=1, has_side_effects=True, vmem_limit_bytes=32 * 1024 * 1024
        ),
    )(local)


def fit_kernel(channels, count, last, both_ref, own_ref, out_ref, gram_slots, seen_slots, work, inv, gathered, sems):
    rank = work.shape[0]
    size, rows = gram_slots.shape[1], seen_slots.shape[1]
    me = lax.axis_index("chan")
    greet("chan", count)
    copy = copier(sems, "chan", count)
    grams = scatter_copies(copy, 0, count, both_ref, 0, size, gram_slots)
    seens = scatter_copies(copy, 1, count, both_ref, rank, rows, seen_slots)
    for one in grams:
        one.start()
    total = both_ref[part(me, size)]
    for one in grams:
        one.wait_recv()
    for d in range(1, count):
        total = total + gram_slots[d - 1]
    work[part(me, size)] = total
    gather_rows(copy, 2, count, work, size)
    for one in seens:
        one.start()

    def block_step(b, carry):
        at = pl.multiple_of(b * B, B)
        invert_block(work[pl.ds(at, B), pl.ds(at, B)], inv.at[b])
        for k in range(rank // B - 1):

            @pl.when(b == k)
            def _():
                lo, hi = k * B, (k + 1) * B
                panel = dot_t(work[hi:, lo:hi], inv[k])
                work[hi:, lo:hi] = panel
                work[hi:, hi:] = work[hi:, hi:] - dot_t(panel, panel)

        return carry

    lax.fori_loop(0, rank // B, block_step, 0)
    for one in seens:
        one.wait_recv()
    seen = both_ref[part(me, rows, rank)]
    for d in range(1, count):
        seen = seen + seen_slots[d - 1]
    solved = []
    for k in range(rank // B):
        lo, hi = k * B, (k + 1) * B
        rest = seen[:, lo:hi]
        if k:
            rest = rest - dot_t(jnp.concatenate(solved, axis=1), work[lo:hi, :lo])
        solved.append(dot_t(rest, inv[k]))
    coords = jnp.concatenate(solved, axis=1)
    own = own_ref[...]
    energy = jnp.maximum(own[:, rank : rank + 1] - jnp.sum(coords * coords, axis=1, keepdims=True), 0.0)
    weights = jnp.minimum(1.0, 3.0 / jnp.sqrt(energy / channels + 1e-06))
    if last:
        gathered[part(me, rows), :rank] = coords
        gathered[part(me, rows), rank:] = jnp.broadcast_to(weights, (rows, B))
    else:
        gathered[part(me, rows)] = ((weights * weights) * own[:, :rank]).astype(jnp.bfloat16)
    gather_rows(copy, 3, count, gathered, rows)
    for one in grams + seens:
        one.wait_send()
    out_ref[...] = gathered[...]


def fit(channels, count, last, both, own):
    size, rank = own.shape[0], both.shape[1]
    rows = size * count
    kept = ((rows, rank + B), jnp.float32) if last else ((rows, rank), jnp.bfloat16)
    return pl.pallas_call(
        functools.partial(fit_kernel, channels, count, last),
        out_shape=jax.ShapeDtypeStruct(*kept),
        scratch_shapes=[
            pltpu.VMEM((count - 1, rank // count, rank), jnp.float32),
            pltpu.VMEM((count - 1, size, rank), jnp.float32),
            pltpu.VMEM((rank, rank), jnp.float32),
            pltpu.VMEM((rank // B, B, B), jnp.float32),
            pltpu.VMEM(*kept),
            pltpu.SemaphoreType.DMA((2, 4, count - 1)),
        ],
        compiler_params=pltpu.CompilerParams(
            collective_id=3 if last else 2, has_side_effects=True, vmem_limit_bytes=32 * 1024 * 1024
        ),
    )(both, own)


def exchange_kernel(outer, inner, mine_ref, samples_ref, both_ref, whole, near, sent, far, acc, near_sem, far_sem, wide_sem, local_sem):
    me = lax.axis_index("tm")
    o, i = me // inner, me % inner
    size, rank = acc.shape
    f32 = jnp.float32

    def peer_in(d):
        return {"tm": o * inner + (i + d) % inner}

    def peer_out(e):
        return {"tm": ((o + e) % outer) * inner + i}

    barrier = pltpu.get_barrier_semaphore()
    for d in range(1, inner):
        pl.semaphore_signal(barrier, inc=1, device_id=peer_in(d), device_id_type=MESH)
    for e in range(1, outer):
        pl.semaphore_signal(barrier, inc=1, device_id=peer_out(e), device_id_type=MESH)
    pl.semaphore_wait(barrier, inner + outer - 2)

    def copy(src, dst, sems, at, device):
        return pltpu.make_async_remote_copy(
            src_ref=src,
            dst_ref=dst,
            send_sem=sems.at[(0,) + at],
            recv_sem=sems.at[(1,) + at],
            device_id=device,
            device_id_type=MESH,
        )

    order = list(range(1, outer)) + [0]
    first = {}
    for e in order:
        row = (o + e) % outer
        for d in range(1, inner):
            block = row * inner + (i + d) % inner
            first[e, d] = copy(mine_ref.at[block], near.at[e, d - 1], near_sem, (e, d - 1), peer_in(d))
            first[e, d].start()
    second = {}
    for e in order:
        for d in range(1, inner):
            first[e, d].wait_recv()
        total = mine_ref[((o + e) % outer) * inner + i].astype(f32)
        for d in range(1, inner):
            total = total + near[e, d - 1].astype(f32)
        if e:
            sent[e - 1] = total.astype(jnp.bfloat16)
            second[e] = copy(sent.at[e - 1], far.at[e - 1], far_sem, (e - 1,), peer_out(e))
            second[e].start()
        else:
            acc[...] = total
    for e in range(1, outer):
        second[e].wait_recv()
        acc[...] = acc[...] + far[e - 1].astype(f32)
    whole[me] = acc[...].astype(jnp.bfloat16)

    def wide(e):
        return copy(whole.at[me], whole.at[me], wide_sem, (e - 1,), peer_out(e))

    def local(e, d):
        block = ((o - e + outer) % outer) * inner + i
        return copy(whole.at[block], whole.at[block], local_sem, (e, d - 1), peer_in(d))

    for e in range(1, outer):
        wide(e).start()
    for d in range(1, inner):
        local(0, d).start()
    both_ref[...] = jnp.zeros_like(both_ref)

    def use(block):
        one = whole[block]
        columns = pl.ds(pl.multiple_of(block * size, size), size)
        both_ref[:rank] += lax.dot_general(one, one, (((0,), (0,)), ((), ())), preferred_element_type=f32)
        both_ref[rank:] += jnp.dot(samples_ref[:, columns], one, preferred_element_type=f32)

    use(me)
    for e in range(1, outer):
        block = ((o - e + outer) % outer) * inner + i
        copy(whole.at[block], whole.at[block], wide_sem, (e - 1,), peer_out(e)).wait_recv()
        for d in range(1, inner):
            local(e, d).start()
        use(block)
    for e in range(outer):
        for d in range(1, inner):
            block = ((o - e + outer) % outer) * inner + (i - d + inner) % inner
            copy(whole.at[block], whole.at[block], local_sem, (e, d - 1), peer_in(d)).wait_recv()
            use(block)
    for one in first.values():
        one.wait_send()
    for one in second.values():
        one.wait_send()
    for e in range(1, outer):
        wide(e).wait_send()
    for e in range(outer):
        for d in range(1, inner):
            local(e, d).wait_send()


def exchange(mine, samples, devices):
    rows, channels = samples.shape
    rank = mine.shape[1]
    outer = 4 if devices % 4 == 0 else 1
    inner = devices // outer
    size = channels // devices
    low = jnp.bfloat16
    return pl.pallas_call(
        functools.partial(exchange_kernel, outer, inner),
        out_shape=jax.ShapeDtypeStruct((rank + rows, rank), jnp.float32),
        in_specs=[pl.BlockSpec(memory_space=pltpu.VMEM)] * 2,
        out_specs=pl.BlockSpec(memory_space=pltpu.VMEM),
        scratch_shapes=[
            pltpu.VMEM((devices, size, rank), low),
            pltpu.VMEM((outer, inner - 1, size, rank), low),
            pltpu.VMEM((outer - 1, size, rank), low),
            pltpu.VMEM((outer - 1, size, rank), low),
            pltpu.VMEM((size, rank), jnp.float32),
            pltpu.SemaphoreType.DMA((2, outer, inner - 1)),
            pltpu.SemaphoreType.DMA((2, outer - 1)),
            pltpu.SemaphoreType.DMA((2, outer - 1)),
            pltpu.SemaphoreType.DMA((2, outer, inner - 1)),
        ],
        compiler_params=pltpu.CompilerParams(
            collective_id=0, has_side_effects=True, vmem_limit_bytes=40 * 1024 * 1024
        ),
    )(mine.reshape(devices, size, rank), samples)


def shards(samples, sketch, channels, devices, count):
    rows, rank = samples.shape[0], sketch.shape[1]
    f32 = jnp.float32
    wide = samples.astype(f32)
    norms = jnp.sum(wide * wide, axis=1)
    local = jnp.dot(samples, sketch, preferred_element_type=f32)
    local = jnp.concatenate([local, jnp.broadcast_to(norms[:, None], (rows, B))], axis=1)
    own, weighted = start(local, rank, count)
    for step in range(ROUNDS):
        local_factor = jnp.einsum("sc,sk->ck", samples, weighted, preferred_element_type=f32)
        both = exchange(local_factor.astype(jnp.bfloat16), samples, devices)
        weighted = fit(channels, count, step == ROUNDS - 1, both, own)
    return (weighted[:, :rank], weighted[:, rank])


def solution(mesh):
    in_specs = (P("tm", "chan"), P("chan", None))
    out_specs = (P("tm", None), P("tm"))

    def whole(samples, sketch):
        f = lambda a, b: shards(a, b, samples.shape[1], mesh.shape["tm"], mesh.shape["chan"])
        return jax.shard_map(f, mesh=mesh, in_specs=in_specs, out_specs=out_specs, check_vma=False)(samples, sketch)

    return whole
```

```python
import functools

import jax
import jax.numpy as jnp
from jax import lax
from jax.experimental import pallas as pl
from jax.experimental.pallas import tpu as pltpu
from jax.sharding import PartitionSpec as P

ROUNDS = 2
B = 128
GROUP = 4
HIGH = lax.Precision.HIGHEST
MESH = pl.DeviceIdType.MESH


def dot_t(a, b):
    return lax.dot_general(a, b, (((1,), (1,)), ((), ())), precision=HIGH, preferred_element_type=jnp.float32)


def invert_block(block, inv_ref):
    eye = lax.broadcasted_iota(jnp.int32, (B, B), 0) == lax.broadcasted_iota(jnp.int32, (B, B), 1)
    left, right = block, eye.astype(jnp.float32)
    top = 0
    for j in range(0, B, GROUP):
        cut = (j // 8) * 8 - top
        if cut:
            left, right, top = left[cut:], right[cut:], top + cut
        k = j - top
        span = range(GROUP)
        rows = [left[k + t : k + t + 1, :] for t in span]
        rights = [right[k + t : k + t + 1, :] for t in span]
        cols = [jnp.broadcast_to(left[:, j + t : j + t + 1], left.shape) for t in span]
        pivot = {
            (u, t): jnp.broadcast_to(left[k + u : k + u + 1, j + t : j + t + 1], (1, B))
            for u in span
            for t in range(u + 1)
        }
        for t in span:
            scale = lax.rsqrt(pivot[t, t])
            rows[t], rights[t], cols[t] = rows[t] * scale, rights[t] * scale, cols[t] * scale
            below = {u: pivot[u, t] * scale for u in range(t + 1, GROUP)}
            for u in below:
                rows[u] = rows[u] - below[u] * rows[t]
                rights[u] = rights[u] - below[u] * rights[t]
                cols[u] = cols[u] - below[u] * cols[t]
                for v in range(t + 1, u + 1):
                    pivot[u, v] = pivot[u, v] - below[u] * below[v]
            inv_ref[j + t : j + t + 1, :] = rights[t]
        if j + GROUP < B:
            for t in span:
                left = left - cols[t] * rows[t]
                right = right - cols[t] * rights[t]


def copier(sems, axis, count):
    me = lax.axis_index(axis)

    def copy(slot, d, src, dst):
        return pltpu.make_async_remote_copy(
            src_ref=src,
            dst_ref=dst,
            send_sem=sems.at[0, slot, d - 1],
            recv_sem=sems.at[1, slot, d - 1],
            device_id={axis: (me + d) % count},
            device_id_type=MESH,
        )

    return copy


def greet(axis, count):
    me = lax.axis_index(axis)
    barrier = pltpu.get_barrier_semaphore()
    for d in range(1, count):
        pl.semaphore_signal(barrier, inc=1, device_id={axis: (me + d) % count}, device_id_type=MESH)
    pl.semaphore_wait(barrier, count - 1)


def part(index, size, base=0):
    return pl.ds(pl.multiple_of(base + index * size, size), size)


def scatter_copies(copy, slot, count, source, base, size, slots):
    me = lax.axis_index("chan")
    return [
        copy(slot, d, source.at[part((me + d) % count, size, base)], slots.at[d - 1]) for d in range(1, count)
    ]


def gather_rows(copy, slot, count, whole, size):
    me = lax.axis_index("chan")
    sends = [copy(slot, d, whole.at[part(me, size)], whole.at[part(me, size)]) for d in range(1, count)]
    for one in sends:
        one.start()
    for d in range(1, count):
        came = whole.at[part((me - d + count) % count, size)]
        copy(slot, d, came, came).wait_recv()
    for one in sends:
        one.wait_send()


def start_kernel(count, local_ref, own_ref, weighted_ref, slots, gathered, sems):
    size, rank = slots.shape[1], weighted_ref.shape[1]
    me = lax.axis_index("chan")
    greet("chan", count)
    copy = copier(sems, "chan", count)
    sends = scatter_copies(copy, 0, count, local_ref, 0, size, slots)
    for one in sends:
        one.start()
    total = local_ref[part(me, size)]
    for one in sends:
        one.wait_recv()
    for d in range(1, count):
        total = total + slots[d - 1]
    own_ref[...] = total
    gathered[part(me, size)] = total[:, :rank].astype(jnp.bfloat16)
    gather_rows(copy, 1, count, gathered, size)
    for one in sends:
        one.wait_send()
    weighted_ref[...] = gathered[...]


def start(local, rank, count):
    rows, wide = local.shape
    size = rows // count
    return pl.pallas_call(
        functools.partial(start_kernel, count),
        out_shape=(
            jax.ShapeDtypeStruct((size, wide), jnp.float32),
            jax.ShapeDtypeStruct((rows, rank), jnp.bfloat16),
        ),
        scratch_shapes=[
            pltpu.VMEM((count - 1, size, wide), jnp.float32),
            pltpu.VMEM((rows, rank), jnp.bfloat16),
            pltpu.SemaphoreType.DMA((2, 2, count - 1)),
        ],
        compiler_params=pltpu.CompilerParams(
            collective_id=1, has_side_effects=True, vmem_limit_bytes=32 * 1024 * 1024
        ),
    )(local)


def fit_kernel(channels, count, last, both_ref, own_ref, out_ref, gram_slots, seen_slots, work, inv, gathered, sems):
    rank = work.shape[0]
    size, rows = gram_slots.shape[1], seen_slots.shape[1]
    me = lax.axis_index("chan")
    greet("chan", count)
    copy = copier(sems, "chan", count)
    grams = scatter_copies(copy, 0, count, both_ref, 0, size, gram_slots)
    seens = scatter_copies(copy, 1, count, both_ref, rank, rows, seen_slots)
    for one in grams:
        one.start()
    total = both_ref[part(me, size)]
    for one in grams:
        one.wait_recv()
    for d in range(1, count):
        total = total + gram_slots[d - 1]
    work[part(me, size)] = total
    gather_rows(copy, 2, count, work, size)
    for one in seens:
        one.start()

    def block_step(b, carry):
        at = pl.multiple_of(b * B, B)
        invert_block(work[pl.ds(at, B), pl.ds(at, B)], inv.at[b])
        for k in range(rank // B - 1):

            @pl.when(b == k)
            def _():
                lo, hi = k * B, (k + 1) * B
                panel = dot_t(work[hi:, lo:hi], inv[k])
                work[hi:, lo:hi] = panel
                work[hi:, hi:] = work[hi:, hi:] - dot_t(panel, panel)

        return carry

    lax.fori_loop(0, rank // B, block_step, 0)
    for one in seens:
        one.wait_recv()
    seen = both_ref[part(me, rows, rank)]
    for d in range(1, count):
        seen = seen + seen_slots[d - 1]
    solved = []
    for k in range(rank // B):
        lo, hi = k * B, (k + 1) * B
        rest = seen[:, lo:hi]
        if k:
            rest = rest - dot_t(jnp.concatenate(solved, axis=1), work[lo:hi, :lo])
        solved.append(dot_t(rest, inv[k]))
    coords = jnp.concatenate(solved, axis=1)
    own = own_ref[...]
    energy = jnp.maximum(own[:, rank : rank + 1] - jnp.sum(coords * coords, axis=1, keepdims=True), 0.0)
    weights = jnp.minimum(1.0, 3.0 / jnp.sqrt(energy / channels + 1e-06))
    if last:
        gathered[part(me, rows), :rank] = coords
        gathered[part(me, rows), rank:] = jnp.broadcast_to(weights, (rows, B))
    else:
        gathered[part(me, rows)] = ((weights * weights) * own[:, :rank]).astype(jnp.bfloat16)
    gather_rows(copy, 3, count, gathered, rows)
    for one in grams + seens:
        one.wait_send()
    out_ref[...] = gathered[...]


def fit(channels, count, last, both, own):
    size, rank = own.shape[0], both.shape[1]
    rows = size * count
    kept = ((rows, rank + B), jnp.float32) if last else ((rows, rank), jnp.bfloat16)
    return pl.pallas_call(
        functools.partial(fit_kernel, channels, count, last),
        out_shape=jax.ShapeDtypeStruct(*kept),
        scratch_shapes=[
            pltpu.VMEM((count - 1, rank // count, rank), jnp.float32),
            pltpu.VMEM((count - 1, size, rank), jnp.float32),
            pltpu.VMEM((rank, rank), jnp.float32),
            pltpu.VMEM((rank // B, B, B), jnp.float32),
            pltpu.VMEM(*kept),
            pltpu.SemaphoreType.DMA((2, 4, count - 1)),
        ],
        compiler_params=pltpu.CompilerParams(
            collective_id=3 if last else 2, has_side_effects=True, vmem_limit_bytes=32 * 1024 * 1024
        ),
    )(both, own)


def exchange_kernel(outer, inner, weighted_ref, samples_ref, both_ref, mine_ref, whole, near, sent, far, acc, near_sem, far_sem, wide_sem, local_sem):
    me = lax.axis_index("tm")
    o, i = me // inner, me % inner
    size, rank = acc.shape
    f32 = jnp.float32

    def peer_in(d):
        return {"tm": o * inner + (i + d) % inner}

    def peer_out(e):
        return {"tm": ((o + e) % outer) * inner + i}

    barrier = pltpu.get_barrier_semaphore()
    for d in range(1, inner):
        pl.semaphore_signal(barrier, inc=1, device_id=peer_in(d), device_id_type=MESH)
    for e in range(1, outer):
        pl.semaphore_signal(barrier, inc=1, device_id=peer_out(e), device_id_type=MESH)
    pl.semaphore_wait(barrier, inner + outer - 2)

    def copy(src, dst, sems, at, device):
        return pltpu.make_async_remote_copy(
            src_ref=src,
            dst_ref=dst,
            send_sem=sems.at[(0,) + at],
            recv_sem=sems.at[(1,) + at],
            device_id=device,
            device_id_type=MESH,
        )

    def factor(block):
        columns = pl.ds(pl.multiple_of(block * size, size), size)
        return lax.dot_general(
            samples_ref[:, columns], weighted_ref[...], (((0,), (0,)), ((), ())), preferred_element_type=f32
        )

    order = list(range(1, outer)) + [0]
    first = {}
    for e in order:
        row = (o + e) % outer
        for d in range(1, inner):
            block = row * inner + (i + d) % inner
            mine_ref[block] = factor(block).astype(jnp.bfloat16)
            first[e, d] = copy(mine_ref.at[block], near.at[e, d - 1], near_sem, (e, d - 1), peer_in(d))
            first[e, d].start()
    second = {}
    for e in order:
        total = factor(((o + e) % outer) * inner + i)
        for d in range(1, inner):
            first[e, d].wait_recv()
        for d in range(1, inner):
            total = total + near[e, d - 1].astype(f32)
        if e:
            sent[e - 1] = total.astype(jnp.bfloat16)
            second[e] = copy(sent.at[e - 1], far.at[e - 1], far_sem, (e - 1,), peer_out(e))
            second[e].start()
        else:
            acc[...] = total
    for e in range(1, outer):
        second[e].wait_recv()
        acc[...] = acc[...] + far[e - 1].astype(f32)
    whole[me] = acc[...].astype(jnp.bfloat16)

    def wide(e):
        return copy(whole.at[me], whole.at[me], wide_sem, (e - 1,), peer_out(e))

    def local(e, d):
        block = ((o - e + outer) % outer) * inner + i
        return copy(whole.at[block], whole.at[block], local_sem, (e, d - 1), peer_in(d))

    for e in range(1, outer):
        wide(e).start()
    for d in range(1, inner):
        local(0, d).start()
    both_ref[...] = jnp.zeros_like(both_ref)

    def use(block):
        one = whole[block]
        columns = pl.ds(pl.multiple_of(block * size, size), size)
        both_ref[:rank] += lax.dot_general(one, one, (((0,), (0,)), ((), ())), preferred_element_type=f32)
        both_ref[rank:] += jnp.dot(samples_ref[:, columns], one, preferred_element_type=f32)

    use(me)
    for e in range(1, outer):
        block = ((o - e + outer) % outer) * inner + i
        copy(whole.at[block], whole.at[block], wide_sem, (e - 1,), peer_out(e)).wait_recv()
        for d in range(1, inner):
            local(e, d).start()
        use(block)
    for e in range(outer):
        for d in range(1, inner):
            block = ((o - e + outer) % outer) * inner + (i - d + inner) % inner
            copy(whole.at[block], whole.at[block], local_sem, (e, d - 1), peer_in(d)).wait_recv()
            use(block)
    for one in first.values():
        one.wait_send()
    for one in second.values():
        one.wait_send()
    for e in range(1, outer):
        wide(e).wait_send()
    for e in range(outer):
        for d in range(1, inner):
            local(e, d).wait_send()


def exchange(weighted, samples, devices):
    rows, channels = samples.shape
    rank = weighted.shape[1]
    outer = 4 if devices % 4 == 0 else 1
    inner = devices // outer
    size = channels // devices
    low = jnp.bfloat16
    return pl.pallas_call(
        functools.partial(exchange_kernel, outer, inner),
        out_shape=jax.ShapeDtypeStruct((rank + rows, rank), jnp.float32),
        in_specs=[pl.BlockSpec(memory_space=pltpu.VMEM)] * 2,
        out_specs=pl.BlockSpec(memory_space=pltpu.VMEM),
        scratch_shapes=[
            pltpu.VMEM((devices, size, rank), low),
            pltpu.VMEM((devices, size, rank), low),
            pltpu.VMEM((outer, inner - 1, size, rank), low),
            pltpu.VMEM((outer - 1, size, rank), low),
            pltpu.VMEM((outer - 1, size, rank), low),
            pltpu.VMEM((size, rank), jnp.float32),
            pltpu.SemaphoreType.DMA((2, outer, inner - 1)),
            pltpu.SemaphoreType.DMA((2, outer - 1)),
            pltpu.SemaphoreType.DMA((2, outer - 1)),
            pltpu.SemaphoreType.DMA((2, outer, inner - 1)),
        ],
        compiler_params=pltpu.CompilerParams(
            collective_id=0, has_side_effects=True, vmem_limit_bytes=40 * 1024 * 1024
        ),
    )(weighted, samples)


def shards(samples, sketch, channels, devices, count):
    rows, rank = samples.shape[0], sketch.shape[1]
    f32 = jnp.float32
    wide = samples.astype(f32)
    norms = jnp.sum(wide * wide, axis=1)
    local = jnp.dot(samples, sketch, preferred_element_type=f32)
    local = jnp.concatenate([local, jnp.broadcast_to(norms[:, None], (rows, B))], axis=1)
    own, weighted = start(local, rank, count)
    for step in range(ROUNDS):
        both = exchange(weighted, samples, devices)
        weighted = fit(channels, count, step == ROUNDS - 1, both, own)
    return (weighted[:, :rank], weighted[:, rank])


def solution(mesh):
    in_specs = (P("tm", "chan"), P("chan", None))
    out_specs = (P("tm", None), P("tm"))

    def whole(samples, sketch):
        f = lambda a, b: shards(a, b, samples.shape[1], mesh.shape["tm"], mesh.shape["chan"])
        return jax.shard_map(f, mesh=mesh, in_specs=in_specs, out_specs=out_specs, check_vma=False)(samples, sketch)

    return whole
```

```python
import functools

import jax
import jax.numpy as jnp
from jax import lax
from jax.experimental import pallas as pl
from jax.experimental.pallas import tpu as pltpu
from jax.sharding import PartitionSpec as P

ROUNDS = 2
B = 128
GROUP = 4
PIECES = 4
HIGH = lax.Precision.HIGHEST
MESH = pl.DeviceIdType.MESH


def dot_t(a, b):
    return lax.dot_general(a, b, (((1,), (1,)), ((), ())), precision=HIGH, preferred_element_type=jnp.float32)


def invert_block(block, inv_ref):
    eye = lax.broadcasted_iota(jnp.int32, (B, B), 0) == lax.broadcasted_iota(jnp.int32, (B, B), 1)
    left, right = block, eye.astype(jnp.float32)
    top = 0
    for j in range(0, B, GROUP):
        cut = (j // 8) * 8 - top
        if cut:
            left, right, top = left[cut:], right[cut:], top + cut
        k = j - top
        span = range(GROUP)
        rows = [left[k + t : k + t + 1, :] for t in span]
        rights = [right[k + t : k + t + 1, :] for t in span]
        cols = [jnp.broadcast_to(left[:, j + t : j + t + 1], left.shape) for t in span]
        pivot = {
            (u, t): jnp.broadcast_to(left[k + u : k + u + 1, j + t : j + t + 1], (1, B))
            for u in span
            for t in range(u + 1)
        }
        for t in span:
            scale = lax.rsqrt(pivot[t, t])
            rows[t], rights[t], cols[t] = rows[t] * scale, rights[t] * scale, cols[t] * scale
            below = {u: pivot[u, t] * scale for u in range(t + 1, GROUP)}
            for u in below:
                rows[u] = rows[u] - below[u] * rows[t]
                rights[u] = rights[u] - below[u] * rights[t]
                cols[u] = cols[u] - below[u] * cols[t]
                for v in range(t + 1, u + 1):
                    pivot[u, v] = pivot[u, v] - below[u] * below[v]
            inv_ref[j + t : j + t + 1, :] = rights[t]
        if j + GROUP < B:
            for t in span:
                left = left - cols[t] * rows[t]
                right = right - cols[t] * rights[t]


def copier(sems, axis, count):
    me = lax.axis_index(axis)

    def copy(slot, d, src, dst):
        return pltpu.make_async_remote_copy(
            src_ref=src,
            dst_ref=dst,
            send_sem=sems.at[0, slot, d - 1],
            recv_sem=sems.at[1, slot, d - 1],
            device_id={axis: (me + d) % count},
            device_id_type=MESH,
        )

    return copy


def greet(axis, count):
    me = lax.axis_index(axis)
    barrier = pltpu.get_barrier_semaphore()
    for d in range(1, count):
        pl.semaphore_signal(barrier, inc=1, device_id={axis: (me + d) % count}, device_id_type=MESH)
    pl.semaphore_wait(barrier, count - 1)


def part(index, size, base=0):
    return pl.ds(pl.multiple_of(base + index * size, size), size)


def scatter_copies(copy, slot, count, source, base, size, slots):
    me = lax.axis_index("chan")
    return [
        copy(slot, d, source.at[part((me + d) % count, size, base)], slots.at[d - 1]) for d in range(1, count)
    ]


def gather_rows(copy, slot, count, whole, size):
    me = lax.axis_index("chan")
    sends = [copy(slot, d, whole.at[part(me, size)], whole.at[part(me, size)]) for d in range(1, count)]
    for one in sends:
        one.start()
    for d in range(1, count):
        came = whole.at[part((me - d + count) % count, size)]
        copy(slot, d, came, came).wait_recv()
    for one in sends:
        one.wait_send()


def start_kernel(count, local_ref, own_ref, weighted_ref, slots, gathered, sems):
    size, rank = slots.shape[1], weighted_ref.shape[1]
    me = lax.axis_index("chan")
    greet("chan", count)
    copy = copier(sems, "chan", count)
    sends = scatter_copies(copy, 0, count, local_ref, 0, size, slots)
    for one in sends:
        one.start()
    total = local_ref[part(me, size)]
    for one in sends:
        one.wait_recv()
    for d in range(1, count):
        total = total + slots[d - 1]
    own_ref[...] = total
    gathered[part(me, size)] = total[:, :rank].astype(jnp.bfloat16)
    gather_rows(copy, 1, count, gathered, size)
    for one in sends:
        one.wait_send()
    weighted_ref[...] = gathered[...]


def start(local, rank, count):
    rows, wide = local.shape
    size = rows // count
    return pl.pallas_call(
        functools.partial(start_kernel, count),
        out_shape=(
            jax.ShapeDtypeStruct((size, wide), jnp.float32),
            jax.ShapeDtypeStruct((rows, rank), jnp.bfloat16),
        ),
        scratch_shapes=[
            pltpu.VMEM((count - 1, size, wide), jnp.float32),
            pltpu.VMEM((rows, rank), jnp.bfloat16),
            pltpu.SemaphoreType.DMA((2, 2, count - 1)),
        ],
        compiler_params=pltpu.CompilerParams(
            collective_id=1, has_side_effects=True, vmem_limit_bytes=32 * 1024 * 1024
        ),
    )(local)


def fit_kernel(channels, count, last, both_ref, own_ref, out_ref, gram_slots, seen_slots, work, inv, gathered, sems):
    rank = work.shape[0]
    size, rows = gram_slots.shape[1], seen_slots.shape[1]
    me = lax.axis_index("chan")
    greet("chan", count)
    copy = copier(sems, "chan", count)
    grams = scatter_copies(copy, 0, count, both_ref, 0, size, gram_slots)
    seens = scatter_copies(copy, 1, count, both_ref, rank, rows, seen_slots)
    for one in grams:
        one.start()
    total = both_ref[part(me, size)]
    for one in grams:
        one.wait_recv()
    for d in range(1, count):
        total = total + gram_slots[d - 1]
    work[part(me, size)] = total
    gather_rows(copy, 2, count, work, size)
    for one in seens:
        one.start()

    def block_step(b, carry):
        at = pl.multiple_of(b * B, B)
        invert_block(work[pl.ds(at, B), pl.ds(at, B)], inv.at[b])
        for k in range(rank // B - 1):

            @pl.when(b == k)
            def _():
                lo, hi = k * B, (k + 1) * B
                panel = dot_t(work[hi:, lo:hi], inv[k])
                work[hi:, lo:hi] = panel
                work[hi:, hi:] = work[hi:, hi:] - dot_t(panel, panel)

        return carry

    lax.fori_loop(0, rank // B, block_step, 0)
    for one in seens:
        one.wait_recv()
    seen = both_ref[part(me, rows, rank)]
    for d in range(1, count):
        seen = seen + seen_slots[d - 1]
    solved = []
    for k in range(rank // B):
        lo, hi = k * B, (k + 1) * B
        rest = seen[:, lo:hi]
        if k:
            rest = rest - dot_t(jnp.concatenate(solved, axis=1), work[lo:hi, :lo])
        solved.append(dot_t(rest, inv[k]))
    coords = jnp.concatenate(solved, axis=1)
    own = own_ref[...]
    energy = jnp.maximum(own[:, rank : rank + 1] - jnp.sum(coords * coords, axis=1, keepdims=True), 0.0)
    weights = jnp.minimum(1.0, 3.0 / jnp.sqrt(energy / channels + 1e-06))
    if last:
        gathered[part(me, rows), :rank] = coords
        gathered[part(me, rows), rank:] = jnp.broadcast_to(weights, (rows, B))
    else:
        gathered[part(me, rows)] = ((weights * weights) * own[:, :rank]).astype(jnp.bfloat16)
    gather_rows(copy, 3, count, gathered, rows)
    for one in grams + seens:
        one.wait_send()
    out_ref[...] = gathered[...]


def fit(channels, count, last, both, own):
    size, rank = own.shape[0], both.shape[1]
    rows = size * count
    kept = ((rows, rank + B), jnp.float32) if last else ((rows, rank), jnp.bfloat16)
    return pl.pallas_call(
        functools.partial(fit_kernel, channels, count, last),
        out_shape=jax.ShapeDtypeStruct(*kept),
        scratch_shapes=[
            pltpu.VMEM((count - 1, rank // count, rank), jnp.float32),
            pltpu.VMEM((count - 1, size, rank), jnp.float32),
            pltpu.VMEM((rank, rank), jnp.float32),
            pltpu.VMEM((rank // B, B, B), jnp.float32),
            pltpu.VMEM(*kept),
            pltpu.SemaphoreType.DMA((2, 4, count - 1)),
        ],
        compiler_params=pltpu.CompilerParams(
            collective_id=3 if last else 2, has_side_effects=True, vmem_limit_bytes=32 * 1024 * 1024
        ),
    )(both, own)


def exchange_kernel(outer, inner, weighted_ref, samples_ref, both_ref, mine_ref, whole, near, sent, far, acc, near_sem, far_sem, wide_sem, local_sem):
    me = lax.axis_index("tm")
    o, i = me // inner, me % inner
    size, rank = acc.shape
    f32 = jnp.float32

    def peer_in(d):
        return {"tm": o * inner + (i + d) % inner}

    def peer_out(e):
        return {"tm": ((o + e) % outer) * inner + i}

    barrier = pltpu.get_barrier_semaphore()
    for d in range(1, inner):
        pl.semaphore_signal(barrier, inc=1, device_id=peer_in(d), device_id_type=MESH)
    for e in range(1, outer):
        pl.semaphore_signal(barrier, inc=1, device_id=peer_out(e), device_id_type=MESH)
    pl.semaphore_wait(barrier, inner + outer - 2)

    def copy(src, dst, sems, at, device):
        return pltpu.make_async_remote_copy(
            src_ref=src,
            dst_ref=dst,
            send_sem=sems.at[(0,) + at],
            recv_sem=sems.at[(1,) + at],
            device_id=device,
            device_id_type=MESH,
        )

    def factor(block):
        columns = pl.ds(pl.multiple_of(block * size, size), size)
        return lax.dot_general(
            samples_ref[:, columns], weighted_ref[...], (((0,), (0,)), ((), ())), preferred_element_type=f32
        )

    order = list(range(1, outer)) + [0]
    first, second = {}, {}

    def begin(e):
        for d in range(1, inner):
            block = ((o + e) % outer) * inner + (i + d) % inner
            mine_ref[block] = factor(block).astype(jnp.bfloat16)
            first[e, d] = copy(mine_ref.at[block], near.at[e, d - 1], near_sem, (e, d - 1), peer_in(d))
            first[e, d].start()

    for e in order[:2]:
        begin(e)
    for at, e in enumerate(order):
        total = factor(((o + e) % outer) * inner + i)
        for d in range(1, inner):
            first[e, d].wait_recv()
        for later in order[at + 2 : at + 3]:
            begin(later)
        for d in range(1, inner):
            total = total + near[e, d - 1].astype(f32)
        if e:
            sent[e - 1] = total.astype(jnp.bfloat16)
            second[e] = copy(sent.at[e - 1], far.at[e - 1], far_sem, (e - 1,), peer_out(e))
            second[e].start()
        else:
            acc[...] = total
    for e in range(1, outer):
        second[e].wait_recv()
        acc[...] = acc[...] + far[e - 1].astype(f32)
    whole[me] = acc[...].astype(jnp.bfloat16)

    step = size // PIECES

    def piece(block, h):
        return whole.at[block, pl.ds(h * step, step)]

    def wide(e, h, block=me):
        return copy(piece(block, h), piece(block, h), wide_sem, (e - 1, h), peer_out(e))

    def local(e, d, h, shift=0):
        block = ((o - e + outer) % outer) * inner + (i - shift + inner) % inner
        return copy(piece(block, h), piece(block, h), local_sem, (e, d - 1, h), peer_in(d))

    for h in range(2):
        for e in range(1, outer):
            wide(e, h).start()
    for h in range(PIECES):
        for d in range(1, inner):
            local(0, d, h).start()
    both_ref[...] = jnp.zeros_like(both_ref)

    def use(block):
        one = whole[block]
        columns = pl.ds(pl.multiple_of(block * size, size), size)
        both_ref[:rank] += lax.dot_general(one, one, (((0,), (0,)), ((), ())), preferred_element_type=f32)
        both_ref[rank:] += jnp.dot(samples_ref[:, columns], one, preferred_element_type=f32)

    use(me)
    for h in range(PIECES):
        for e in range(1, outer):
            block = ((o - e + outer) % outer) * inner + i
            wide(e, h, block).wait_recv()
            if h + 2 < PIECES:
                wide(e, h + 2).start()
            for d in range(1, inner):
                local(e, d, h).start()
    for e in range(1, outer):
        use(((o - e + outer) % outer) * inner + i)
    for e in range(outer):
        for d in range(1, inner):
            for h in range(PIECES):
                local(e, d, h, d).wait_recv()
            use(((o - e + outer) % outer) * inner + (i - d + inner) % inner)
    for one in first.values():
        one.wait_send()
    for one in second.values():
        one.wait_send()
    for h in range(PIECES):
        for e in range(1, outer):
            wide(e, h).wait_send()
        for e in range(outer):
            for d in range(1, inner):
                local(e, d, h).wait_send()


def exchange(weighted, samples, devices):
    rows, channels = samples.shape
    rank = weighted.shape[1]
    outer = 4 if devices % 4 == 0 else 1
    inner = devices // outer
    size = channels // devices
    low = jnp.bfloat16
    return pl.pallas_call(
        functools.partial(exchange_kernel, outer, inner),
        out_shape=jax.ShapeDtypeStruct((rank + rows, rank), jnp.float32),
        in_specs=[pl.BlockSpec(memory_space=pltpu.VMEM)] * 2,
        out_specs=pl.BlockSpec(memory_space=pltpu.VMEM),
        scratch_shapes=[
            pltpu.VMEM((devices, size, rank), low),
            pltpu.VMEM((devices, size, rank), low),
            pltpu.VMEM((outer, inner - 1, size, rank), low),
            pltpu.VMEM((outer - 1, size, rank), low),
            pltpu.VMEM((outer - 1, size, rank), low),
            pltpu.VMEM((size, rank), jnp.float32),
            pltpu.SemaphoreType.DMA((2, outer, inner - 1)),
            pltpu.SemaphoreType.DMA((2, outer - 1)),
            pltpu.SemaphoreType.DMA((2, outer - 1, PIECES)),
            pltpu.SemaphoreType.DMA((2, outer, inner - 1, PIECES)),
        ],
        compiler_params=pltpu.CompilerParams(
            collective_id=0, has_side_effects=True, vmem_limit_bytes=40 * 1024 * 1024
        ),
    )(weighted, samples)


def shards(samples, sketch, channels, devices, count):
    rows, rank = samples.shape[0], sketch.shape[1]
    f32 = jnp.float32
    wide = samples.astype(f32)
    norms = jnp.sum(wide * wide, axis=1)
    local = jnp.dot(samples, sketch, preferred_element_type=f32)
    local = jnp.concatenate([local, jnp.broadcast_to(norms[:, None], (rows, B))], axis=1)
    own, weighted = start(local, rank, count)
    for step in range(ROUNDS):
        both = exchange(weighted, samples, devices)
        weighted = fit(channels, count, step == ROUNDS - 1, both, own)
    return (weighted[:, :rank], weighted[:, rank])


def solution(mesh):
    in_specs = (P("tm", "chan"), P("chan", None))
    out_specs = (P("tm", None), P("tm"))

    def whole(samples, sketch):
        f = lambda a, b: shards(a, b, samples.shape[1], mesh.shape["tm"], mesh.shape["chan"])
        return jax.shard_map(f, mesh=mesh, in_specs=in_specs, out_specs=out_specs, check_vma=False)(samples, sketch)

    return whole
```

```python
import functools

import jax
import jax.numpy as jnp
from jax import lax
from jax.experimental import pallas as pl
from jax.experimental.pallas import tpu as pltpu
from jax.sharding import PartitionSpec as P

ROUNDS = 2
B = 128
GROUP = 4
PIECES = 8
HIGH = lax.Precision.HIGHEST
MESH = pl.DeviceIdType.MESH


def dot_t(a, b):
    return lax.dot_general(a, b, (((1,), (1,)), ((), ())), precision=HIGH, preferred_element_type=jnp.float32)


def invert_block(block, inv_ref):
    eye = lax.broadcasted_iota(jnp.int32, (B, B), 0) == lax.broadcasted_iota(jnp.int32, (B, B), 1)
    left, right = block, eye.astype(jnp.float32)
    top = 0
    for j in range(0, B, GROUP):
        cut = (j // 8) * 8 - top
        if cut:
            left, right, top = left[cut:], right[cut:], top + cut
        k = j - top
        span = range(GROUP)
        rows = [left[k + t : k + t + 1, :] for t in span]
        rights = [right[k + t : k + t + 1, :] for t in span]
        cols = [jnp.broadcast_to(left[:, j + t : j + t + 1], left.shape) for t in span]
        pivot = {
            (u, t): jnp.broadcast_to(left[k + u : k + u + 1, j + t : j + t + 1], (1, B))
            for u in span
            for t in range(u + 1)
        }
        for t in span:
            scale = lax.rsqrt(pivot[t, t])
            rows[t], rights[t], cols[t] = rows[t] * scale, rights[t] * scale, cols[t] * scale
            below = {u: pivot[u, t] * scale for u in range(t + 1, GROUP)}
            for u in below:
                rows[u] = rows[u] - below[u] * rows[t]
                rights[u] = rights[u] - below[u] * rights[t]
                cols[u] = cols[u] - below[u] * cols[t]
                for v in range(t + 1, u + 1):
                    pivot[u, v] = pivot[u, v] - below[u] * below[v]
            inv_ref[j + t : j + t + 1, :] = rights[t]
        if j + GROUP < B:
            for t in span:
                left = left - cols[t] * rows[t]
                right = right - cols[t] * rights[t]


def copier(sems, axis, count):
    me = lax.axis_index(axis)

    def copy(slot, d, src, dst):
        return pltpu.make_async_remote_copy(
            src_ref=src,
            dst_ref=dst,
            send_sem=sems.at[0, slot, d - 1],
            recv_sem=sems.at[1, slot, d - 1],
            device_id={axis: (me + d) % count},
            device_id_type=MESH,
        )

    return copy


def greet(axis, count):
    me = lax.axis_index(axis)
    barrier = pltpu.get_barrier_semaphore()
    for d in range(1, count):
        pl.semaphore_signal(barrier, inc=1, device_id={axis: (me + d) % count}, device_id_type=MESH)
    pl.semaphore_wait(barrier, count - 1)


def part(index, size, base=0):
    return pl.ds(pl.multiple_of(base + index * size, size), size)


def scatter_copies(copy, slot, count, source, base, size, slots):
    me = lax.axis_index("chan")
    return [
        copy(slot, d, source.at[part((me + d) % count, size, base)], slots.at[d - 1]) for d in range(1, count)
    ]


def gather_rows(copy, slot, count, whole, size):
    me = lax.axis_index("chan")
    sends = [copy(slot, d, whole.at[part(me, size)], whole.at[part(me, size)]) for d in range(1, count)]
    for one in sends:
        one.start()
    for d in range(1, count):
        came = whole.at[part((me - d + count) % count, size)]
        copy(slot, d, came, came).wait_recv()
    for one in sends:
        one.wait_send()


def start_kernel(count, local_ref, own_ref, weighted_ref, slots, gathered, sems):
    size, rank = slots.shape[1], weighted_ref.shape[1]
    me = lax.axis_index("chan")
    greet("chan", count)
    copy = copier(sems, "chan", count)
    sends = scatter_copies(copy, 0, count, local_ref, 0, size, slots)
    for one in sends:
        one.start()
    total = local_ref[part(me, size)]
    for one in sends:
        one.wait_recv()
    for d in range(1, count):
        total = total + slots[d - 1]
    own_ref[...] = total
    gathered[part(me, size)] = total[:, :rank].astype(jnp.bfloat16)
    gather_rows(copy, 1, count, gathered, size)
    for one in sends:
        one.wait_send()
    weighted_ref[...] = gathered[...]


def start(local, rank, count):
    rows, wide = local.shape
    size = rows // count
    return pl.pallas_call(
        functools.partial(start_kernel, count),
        out_shape=(
            jax.ShapeDtypeStruct((size, wide), jnp.float32),
            jax.ShapeDtypeStruct((rows, rank), jnp.bfloat16),
        ),
        scratch_shapes=[
            pltpu.VMEM((count - 1, size, wide), jnp.float32),
            pltpu.VMEM((rows, rank), jnp.bfloat16),
            pltpu.SemaphoreType.DMA((2, 2, count - 1)),
        ],
        compiler_params=pltpu.CompilerParams(
            collective_id=1, has_side_effects=True, vmem_limit_bytes=32 * 1024 * 1024
        ),
    )(local)


def fit_kernel(channels, count, last, both_ref, own_ref, out_ref, gram_slots, seen_slots, work, inv, gathered, sems):
    rank = work.shape[0]
    size, rows = gram_slots.shape[1], seen_slots.shape[1]
    me = lax.axis_index("chan")
    greet("chan", count)
    copy = copier(sems, "chan", count)
    grams = scatter_copies(copy, 0, count, both_ref, 0, size, gram_slots)
    seens = scatter_copies(copy, 1, count, both_ref, rank, rows, seen_slots)
    for one in grams:
        one.start()
    total = both_ref[part(me, size)]
    for one in grams:
        one.wait_recv()
    for d in range(1, count):
        total = total + gram_slots[d - 1]
    work[part(me, size)] = total
    gather_rows(copy, 2, count, work, size)
    for one in seens:
        one.start()

    def block_step(b, carry):
        at = pl.multiple_of(b * B, B)
        invert_block(work[pl.ds(at, B), pl.ds(at, B)], inv.at[b])
        for k in range(rank // B - 1):

            @pl.when(b == k)
            def _():
                lo, hi = k * B, (k + 1) * B
                panel = dot_t(work[hi:, lo:hi], inv[k])
                work[hi:, lo:hi] = panel
                work[hi:, hi:] = work[hi:, hi:] - dot_t(panel, panel)

        return carry

    lax.fori_loop(0, rank // B, block_step, 0)
    for one in seens:
        one.wait_recv()
    seen = both_ref[part(me, rows, rank)]
    for d in range(1, count):
        seen = seen + seen_slots[d - 1]
    solved = []
    for k in range(rank // B):
        lo, hi = k * B, (k + 1) * B
        rest = seen[:, lo:hi]
        if k:
            rest = rest - dot_t(jnp.concatenate(solved, axis=1), work[lo:hi, :lo])
        solved.append(dot_t(rest, inv[k]))
    coords = jnp.concatenate(solved, axis=1)
    own = own_ref[...]
    energy = jnp.maximum(own[:, rank : rank + 1] - jnp.sum(coords * coords, axis=1, keepdims=True), 0.0)
    weights = jnp.minimum(1.0, 3.0 / jnp.sqrt(energy / channels + 1e-06))
    if last:
        gathered[part(me, rows), :rank] = coords
        gathered[part(me, rows), rank:] = jnp.broadcast_to(weights, (rows, B))
    else:
        gathered[part(me, rows)] = ((weights * weights) * own[:, :rank]).astype(jnp.bfloat16)
    gather_rows(copy, 3, count, gathered, rows)
    for one in grams + seens:
        one.wait_send()
    out_ref[...] = gathered[...]


def fit(channels, count, last, both, own):
    size, rank = own.shape[0], both.shape[1]
    rows = size * count
    kept = ((rows, rank + B), jnp.float32) if last else ((rows, rank), jnp.bfloat16)
    return pl.pallas_call(
        functools.partial(fit_kernel, channels, count, last),
        out_shape=jax.ShapeDtypeStruct(*kept),
        scratch_shapes=[
            pltpu.VMEM((count - 1, rank // count, rank), jnp.float32),
            pltpu.VMEM((count - 1, size, rank), jnp.float32),
            pltpu.VMEM((rank, rank), jnp.float32),
            pltpu.VMEM((rank // B, B, B), jnp.float32),
            pltpu.VMEM(*kept),
            pltpu.SemaphoreType.DMA((2, 4, count - 1)),
        ],
        compiler_params=pltpu.CompilerParams(
            collective_id=3 if last else 2, has_side_effects=True, vmem_limit_bytes=32 * 1024 * 1024
        ),
    )(both, own)


def exchange_kernel(outer, inner, weighted_ref, samples_ref, both_ref, mine_ref, whole, near, sent, far, acc, near_sem, far_sem, wide_sem, local_sem):
    me = lax.axis_index("tm")
    o, i = me // inner, me % inner
    size, rank = acc.shape
    f32 = jnp.float32

    def peer_in(d):
        return {"tm": o * inner + (i + d) % inner}

    def peer_out(e):
        return {"tm": ((o + e) % outer) * inner + i}

    barrier = pltpu.get_barrier_semaphore()
    for d in range(1, inner):
        pl.semaphore_signal(barrier, inc=1, device_id=peer_in(d), device_id_type=MESH)
    for e in range(1, outer):
        pl.semaphore_signal(barrier, inc=1, device_id=peer_out(e), device_id_type=MESH)
    pl.semaphore_wait(barrier, inner + outer - 2)

    def copy(src, dst, sems, at, device):
        return pltpu.make_async_remote_copy(
            src_ref=src,
            dst_ref=dst,
            send_sem=sems.at[(0,) + at],
            recv_sem=sems.at[(1,) + at],
            device_id=device,
            device_id_type=MESH,
        )

    def factor(block):
        columns = pl.ds(pl.multiple_of(block * size, size), size)
        return lax.dot_general(
            samples_ref[:, columns], weighted_ref[...], (((0,), (0,)), ((), ())), preferred_element_type=f32
        )

    order = list(range(1, outer)) + [0]
    first, second = {}, {}

    def begin(e):
        for d in range(1, inner):
            block = ((o + e) % outer) * inner + (i + d) % inner
            mine_ref[block] = factor(block).astype(jnp.bfloat16)
            first[e, d] = copy(mine_ref.at[block], near.at[e, d - 1], near_sem, (e, d - 1), peer_in(d))
            first[e, d].start()

    for e in order[:2]:
        begin(e)
    for at, e in enumerate(order):
        total = factor(((o + e) % outer) * inner + i)
        for d in range(1, inner):
            first[e, d].wait_recv()
        for later in order[at + 2 : at + 3]:
            begin(later)
        for d in range(1, inner):
            total = total + near[e, d - 1].astype(f32)
        if e:
            sent[e - 1] = total.astype(jnp.bfloat16)
            second[e] = copy(sent.at[e - 1], far.at[e - 1], far_sem, (e - 1,), peer_out(e))
            second[e].start()
        else:
            acc[...] = total
    for e in range(1, outer):
        second[e].wait_recv()
        acc[...] = acc[...] + far[e - 1].astype(f32)
    whole[me] = acc[...].astype(jnp.bfloat16)

    step = size // PIECES

    def piece(block, h):
        return whole.at[block, pl.ds(h * step, step)]

    def wide(e, h, block=me):
        return copy(piece(block, h), piece(block, h), wide_sem, (e - 1, h), peer_out(e))

    def local(e, d, h, shift=0):
        block = ((o - e + outer) % outer) * inner + (i - shift + inner) % inner
        return copy(piece(block, h), piece(block, h), local_sem, (e, d - 1, h), peer_in(d))

    for h in range(2):
        for e in range(1, outer):
            wide(e, h).start()
    for h in range(PIECES):
        for d in range(1, inner):
            local(0, d, h).start()
    both_ref[...] = jnp.zeros_like(both_ref)

    def use(block):
        one = whole[block]
        columns = pl.ds(pl.multiple_of(block * size, size), size)
        both_ref[:rank] += lax.dot_general(one, one, (((0,), (0,)), ((), ())), preferred_element_type=f32)
        both_ref[rank:] += jnp.dot(samples_ref[:, columns], one, preferred_element_type=f32)

    use(me)
    for h in range(PIECES):
        for e in range(1, outer):
            block = ((o - e + outer) % outer) * inner + i
            wide(e, h, block).wait_recv()
            if h + 2 < PIECES:
                wide(e, h + 2).start()
            for d in range(1, inner):
                local(e, d, h).start()
    for e in range(1, outer):
        use(((o - e + outer) % outer) * inner + i)
    for e in range(outer):
        for d in range(1, inner):
            for h in range(PIECES):
                local(e, d, h, d).wait_recv()
            use(((o - e + outer) % outer) * inner + (i - d + inner) % inner)
    for one in first.values():
        one.wait_send()
    for one in second.values():
        one.wait_send()
    for h in range(PIECES):
        for e in range(1, outer):
            wide(e, h).wait_send()
        for e in range(outer):
            for d in range(1, inner):
                local(e, d, h).wait_send()


def exchange(weighted, samples, devices):
    rows, channels = samples.shape
    rank = weighted.shape[1]
    outer = 4 if devices % 4 == 0 else 1
    inner = devices // outer
    size = channels // devices
    low = jnp.bfloat16
    return pl.pallas_call(
        functools.partial(exchange_kernel, outer, inner),
        out_shape=jax.ShapeDtypeStruct((rank + rows, rank), jnp.float32),
        in_specs=[pl.BlockSpec(memory_space=pltpu.VMEM)] * 2,
        out_specs=pl.BlockSpec(memory_space=pltpu.VMEM),
        scratch_shapes=[
            pltpu.VMEM((devices, size, rank), low),
            pltpu.VMEM((devices, size, rank), low),
            pltpu.VMEM((outer, inner - 1, size, rank), low),
            pltpu.VMEM((outer - 1, size, rank), low),
            pltpu.VMEM((outer - 1, size, rank), low),
            pltpu.VMEM((size, rank), jnp.float32),
            pltpu.SemaphoreType.DMA((2, outer, inner - 1)),
            pltpu.SemaphoreType.DMA((2, outer - 1)),
            pltpu.SemaphoreType.DMA((2, outer - 1, PIECES)),
            pltpu.SemaphoreType.DMA((2, outer, inner - 1, PIECES)),
        ],
        compiler_params=pltpu.CompilerParams(
            collective_id=0, has_side_effects=True, vmem_limit_bytes=40 * 1024 * 1024
        ),
    )(weighted, samples)


def shards(samples, sketch, channels, devices, count):
    rows, rank = samples.shape[0], sketch.shape[1]
    f32 = jnp.float32
    wide = samples.astype(f32)
    norms = jnp.sum(wide * wide, axis=1)
    local = jnp.dot(samples, sketch, preferred_element_type=f32)
    local = jnp.concatenate([local, jnp.broadcast_to(norms[:, None], (rows, B))], axis=1)
    own, weighted = start(local, rank, count)
    for step in range(ROUNDS):
        both = exchange(weighted, samples, devices)
        weighted = fit(channels, count, step == ROUNDS - 1, both, own)
    return (weighted[:, :rank], weighted[:, rank])


def solution(mesh):
    in_specs = (P("tm", "chan"), P("chan", None))
    out_specs = (P("tm", None), P("tm"))

    def whole(samples, sketch):
        f = lambda a, b: shards(a, b, samples.shape[1], mesh.shape["tm"], mesh.shape["chan"])
        return jax.shard_map(f, mesh=mesh, in_specs=in_specs, out_specs=out_specs, check_vma=False)(samples, sketch)

    return whole
```
